32 devices in a mesh: segment: 4 (over z), mp: 4 (over y, core), tok: 2 (over x).
Axes of the slice: x: 2, y: 2, z: 4, core: 2. Of those that a mesh axis runs over, the one named last changes fastest.
Arguments:
- weights_in: bfloat16 [4, 2, 512, 32768], P('segment', None, None, 'mp'), may hold values from -0.25 to 0.25
- weights_out: bfloat16 [4, 2, 32768, 512], P('segment', None, 'mp'), may hold values from -0.03125 to 0.03125
- norm_gains: float32 [4, 2, 512], P('segment'), may hold values from 0.5 to 1.5
- activations: bfloat16 [4, 2, 2, 256, 512], P('segment', None, 'tok', 'mp'), may hold values from -6 to 6
- gradients: bfloat16 [4, 2, 2, 256, 512], P('segment', None, 'tok', 'mp'), may hold values from -6 to 6
- fresh_inputs: bfloat16 [1, 2, 256, 512], P(None, 'tok', 'mp'), may hold values from -6 to 6
- fresh_gradients: bfloat16 [1, 2, 256, 512], P(None, 'tok', 'mp'), may hold values from -6 to 6
- stashed_inputs: bfloat16 [2, 4, 2, 2, 256, 512], P(None, 'segment', None, 'tok', 'mp'), may hold values from -6 to 6
- stashed_preact: bfloat16 [2, 4, 2, 2, 256, 32768], P(None, 'segment', None, 'tok', None, 'mp'), may hold values from -6 to 6
Outputs:
- leaving_acts: bfloat16 [2, 4, 2, 2, 256, 512], P(None, 'segment', None, 'tok', 'mp')
- leaving_grads: bfloat16 [2, 4, 2, 2, 256, 512], P(None, 'segment', None, 'tok', 'mp')
The draws below stay inside these ranges and needn't reach their ends.
All inputs are finite; a program needn't handle non-finite values.
Results may differ from the reference program's by a relative error of at most 0.014.
Values may be sent and summed in bfloat16 or wider, within the bound.
A program may use at most 128 MiB of HBM per device.

```python
import jax
import jax.numpy as jnp
from jax import lax

D = 512
FF = 32768
TOK_DEV = 256
TICKS = 2
SEGMENTS = 4
HALVES = 2


def levels(stream_key, dims, cuts, smallest, top_value):
    gain = 1.0
    for position, blocks in cuts:
        heights = jax.random.uniform(jax.random.fold_in(jax.random.fold_in(stream_key, 6), position), (blocks,), jnp.float32, smallest / len(cuts), top_value / len(cuts))
        gain = gain * jnp.repeat(jnp.exp(heights), dims[position] // blocks).reshape((-1,) + (1,) * (len(dims) - 1 - position))
    return gain


def bell_draw(own_key, extent, scale, most, cuts=(), held_as=jnp.bfloat16):
    gain = levels(own_key, extent, cuts, -0.22, 0.18) if cuts else 1.0
    values = jax.random.normal(own_key, extent, jnp.float32) * scale * gain
    return jnp.minimum(jnp.maximum(values, -most), most).astype(held_as)


def setup_inputs(seed: int = 0) -> dict:
    key_list = jax.random.split(jax.random.key(seed), 10)
    return {
        "weights_in": bell_draw(key_list[0], (SEGMENTS, 2, D, FF), D ** -0.5, 0.25, ((0, 4), (3, 4))),
        "weights_out": bell_draw(key_list[1], (SEGMENTS, 2, FF, D), FF ** -0.5, 0.03125, ((0, 4), (2, 4))),
        "norm_gains": jnp.clip(0.5 + 1.0 * jax.random.uniform(key_list[2], (SEGMENTS, 2, D), jnp.float32) ** levels(key_list[2], (SEGMENTS, 2, D), ((0, 4),), -0.2, 0.2), 0.5, 1.5),
        "activations": bell_draw(key_list[3], (SEGMENTS, 2, HALVES, TOK_DEV, D), 1.0, 6.0, ((0, 4), (2, 2), (3, 4))),
        "gradients": bell_draw(key_list[4], (SEGMENTS, 2, HALVES, TOK_DEV, D), 1.0, 6.0, ((0, 4), (2, 2), (3, 4))),
        "fresh_inputs": bell_draw(key_list[5], (TICKS - 1, HALVES, TOK_DEV, D), 1.0, 6.0, ((1, 2), (2, 4))),
        "fresh_gradients": bell_draw(key_list[6], (TICKS - 1, HALVES, TOK_DEV, D), 1.0, 6.0, ((1, 2), (2, 4))),
        "stashed_inputs": bell_draw(key_list[7], (TICKS, SEGMENTS, 2, HALVES, TOK_DEV, D), 1.0, 6.0, ((1, 4), (3, 2), (4, 4))),
        "stashed_preact": bell_draw(key_list[8], (TICKS, SEGMENTS, 2, HALVES, TOK_DEV, FF), 1.0, 6.0, ((1, 4), (3, 2), (5, 4))),
    }


epsilon = 1e-06

def normalize(values, gain_row):
    values_wide = values.astype(jnp.float32)
    inverse = lax.rsqrt(lax.optimization_barrier(jnp.mean(values_wide * values_wide, axis=-1, keepdims=True)) + epsilon)
    return values_wide * inverse * gain_row

def forward_layer(rows, gain_row, weight_in, weight_out):
    flat = rows.reshape(-1, rows.shape[-1])
    normed = normalize(flat, gain_row).astype(jnp.bfloat16)
    hidden = jax.nn.relu(jnp.dot(normed, weight_in, preferred_element_type=jnp.float32)).astype(jnp.bfloat16)
    summed = flat.astype(jnp.float32) + jnp.dot(hidden, weight_out, preferred_element_type=jnp.float32)
    return summed.astype(jnp.bfloat16).reshape(rows.shape)

def norm_backward(gradient, stashed, gain_row, norm_grad):
    stashed_wide = stashed.astype(jnp.float32)
    inverse = lax.rsqrt(lax.optimization_barrier(jnp.mean(stashed_wide * stashed_wide, axis=-1, keepdims=True)) + epsilon)
    scaled = gain_row * norm_grad
    inner_sum = lax.optimization_barrier(jnp.mean(stashed_wide * scaled, axis=-1, keepdims=True))
    result = gradient.astype(jnp.float32) + inverse * scaled - stashed_wide * inverse * inverse * inverse * inner_sum
    return result.astype(jnp.bfloat16)

def backward_layer(gradient, stashed, stash_pre, gain_row, weight_in, weight_out):
    flat_grad = gradient.reshape(-1, gradient.shape[-1])
    flat_stash = stashed.reshape(-1, stashed.shape[-1])
    flat_pre = stash_pre.reshape(-1, stash_pre.shape[-1])
    upward = jnp.dot(flat_grad, weight_out.T, preferred_element_type=jnp.float32)
    masked = jnp.where(flat_pre > 0, upward, jnp.zeros_like(upward)).astype(jnp.bfloat16)
    norm_grad = jnp.dot(masked, weight_in.T, preferred_element_type=jnp.float32)
    return norm_backward(flat_grad, flat_stash, gain_row, norm_grad).reshape(gradient.shape)

def reference(weights_in, weights_out, norm_gains, activations, gradients, fresh_inputs, fresh_gradients, stashed_inputs, stashed_preact):
    acts_now = activations
    grads_now = gradients
    forward_ticks = []
    backward_ticks = []
    for tick_index in range(TICKS):
        forward_rows = []
        backward_rows = []
        for section in range(SEGMENTS):
            forward_legs = []
            backward_legs = []
            for leg_index in range(2):
                forward_legs.append(forward_layer(acts_now[section, leg_index], norm_gains[section, leg_index], weights_in[section, leg_index], weights_out[section, leg_index]))
                backward_legs.append(backward_layer(grads_now[section, leg_index], stashed_inputs[tick_index, section, leg_index], stashed_preact[tick_index, section, leg_index], norm_gains[section, leg_index], weights_in[section, leg_index], weights_out[section, leg_index]))
            forward_rows.append(jnp.stack(forward_legs))
            backward_rows.append(jnp.stack(backward_legs))
        forward_all = jnp.stack(forward_rows)
        backward_all = jnp.stack(backward_rows)
        forward_ticks.append(forward_all)
        backward_ticks.append(backward_all)
        if tick_index + 1 < TICKS:
            descent = jnp.concatenate([fresh_inputs[tick_index][None], forward_all[:-1, 0]], axis=0)
            ascent = jnp.concatenate([forward_all[1:, 1], forward_all[-1:, 0]], axis=0)
            acts_now = jnp.stack([descent, ascent], axis=1)
            grad_ascent = jnp.concatenate([fresh_gradients[tick_index][None], backward_all[:-1, 1]], axis=0)
            grad_descent = jnp.concatenate([backward_all[1:, 0], backward_all[-1:, 1]], axis=0)
            grads_now = jnp.stack([grad_descent, grad_ascent], axis=1)
    return (jnp.stack(forward_ticks), jnp.stack(backward_ticks))
```

```python
import functools

import jax
import jax.numpy as jnp
from jax import lax
from jax.experimental import pallas as pl
from jax.experimental.pallas import tpu as pltpu
from jax.sharding import PartitionSpec as P

MESH = pl.DeviceIdType.MESH
EPS = 1e-06
TILE = 1024
ORDER = ((True, 0), (False, 0), (False, 1), (True, 1))
F0, B0, B1, F1 = range(4)


def normalize(values, gain_row):
    wide = values.astype(jnp.float32)
    inverse = lax.rsqrt(jnp.mean(wide * wide, axis=-1, keepdims=True) + EPS)
    return (wide * inverse * gain_row).astype(jnp.bfloat16)


def norm_backward(gradient, stashed, gain_row, norm_grad):
    wide = stashed.astype(jnp.float32)
    inverse = lax.rsqrt(jnp.mean(wide * wide, axis=-1, keepdims=True) + EPS)
    scaled = gain_row * norm_grad
    inner = jnp.mean(wide * scaled, axis=-1, keepdims=True)
    result = gradient.astype(jnp.float32) + inverse * scaled - wide * (inverse * inverse * inverse * inner)
    return result.astype(jnp.bfloat16)


def kernel(
    n, sections, ticks, tiles, tile,
    w_in_hbm, w_out_hbm, gains_hbm, acts_hbm, grads_hbm, fresh_a_hbm, fresh_g_hbm, stash_hbm, pre_hbm,
    out_a_hbm, out_g_hbm,
    w_in, w_out, pre, gains, rows_in, fresh, stash,
    gather, acc, s1_send, s1_recv, s2_send, s2_recv, outs, hop,
    w_sem, pre_sem, small_sem, ag_ssem, ag_rsem, s1_ssem, s1_rsem, s2_ssem, s2_rsem, hop_ssem, hop_rsem, out_sem,
):
    me = lax.axis_index("mp")
    seg = lax.axis_index("segment")
    core = lax.rem(me, 2)
    chip = me // 2
    chips = n // 2
    partner = chip * 2 + (1 - core)
    is_first = seg == 0
    is_last = seg == sections - 1
    r = rows_in.shape[2]
    passes = 4 * ticks

    def rows(block):
        return pl.ds(pl.multiple_of(block * r, r), r)

    small = [
        pltpu.make_async_copy(acts_hbm, rows_in.at[0], small_sem.at[0]),
        pltpu.make_async_copy(gains_hbm, gains, small_sem.at[1]),
        pltpu.make_async_copy(grads_hbm, rows_in.at[1], small_sem.at[2]),
        pltpu.make_async_copy(stash_hbm, stash, small_sem.at[3]),
        pltpu.make_async_copy(fresh_a_hbm, fresh.at[0], small_sem.at[4]),
        pltpu.make_async_copy(fresh_g_hbm, fresh.at[1], small_sem.at[5]),
    ]

    def w_copies(leg, i):
        cut = pl.ds(pl.multiple_of(i * tile, tile), tile)
        return (
            pltpu.make_async_copy(w_in_hbm.at[leg, :, cut], w_in.at[leg, i], w_sem.at[0, leg, i]),
            pltpu.make_async_copy(w_out_hbm.at[leg, cut, :], w_out.at[leg, i], w_sem.at[1, leg, i]),
        )

    def pre_copy(t, leg, i):
        cut = pl.ds(pl.multiple_of(i * tile, tile), tile)
        return pltpu.make_async_copy(pre_hbm.at[t, leg, :, cut], pre.at[2 * t + leg, i], pre_sem.at[2 * t + leg, i])

    small[0].start()
    small[1].start()
    small[2].start()
    for i in range(tiles):
        for copy in w_copies(0, i):
            copy.start()
    for copy in small[3:]:
        copy.start()

    barrier = pltpu.get_barrier_semaphore()
    for d in range(1, n):
        pl.semaphore_signal(barrier, inc=1, device_id={"mp": lax.rem(me + d, n)}, device_id_type=MESH)

    @pl.when(seg > 0)
    def _():
        pl.semaphore_signal(barrier, inc=1, device_id={"segment": seg - 1}, device_id_type=MESH)

    @pl.when(seg < sections - 1)
    def _():
        pl.semaphore_signal(barrier, inc=1, device_id={"segment": seg + 1}, device_id_type=MESH)

    peers = n - 1 + (seg > 0).astype(jnp.int32) + (seg < sections - 1).astype(jnp.int32)
    pl.semaphore_wait(barrier, peers)

    def ag_copy(p, d):
        return pltpu.make_async_remote_copy(
            src_ref=gather.at[p, rows(me)], dst_ref=gather.at[p, rows(me)],
            send_sem=ag_ssem.at[p, d - 1], recv_sem=ag_rsem.at[p, d - 1],
            device_id={"mp": lax.rem(me + d, n)}, device_id_type=MESH,
        )

    def s1_copy(p):
        return pltpu.make_async_remote_copy(
            src_ref=s1_send.at[p], dst_ref=s1_recv.at[p],
            send_sem=s1_ssem.at[p], recv_sem=s1_rsem.at[p],
            device_id={"mp": partner}, device_id_type=MESH,
        )

    def s2_copy(p, d):
        return pltpu.make_async_remote_copy(
            src_ref=s2_send.at[p, d - 1], dst_ref=s2_recv.at[p, d - 1],
            send_sem=s2_ssem.at[p, d - 1], recv_sem=s2_rsem.at[p, d - 1],
            device_id={"mp": lax.rem(chip + d, chips) * 2 + core}, device_id_type=MESH,
        )

    def hop_copy(p):
        step = 1 if p % 4 in (F0, B1) else -1
        return pltpu.make_async_remote_copy(
            src_ref=outs.at[p], dst_ref=hop.at[p],
            send_sem=hop_ssem.at[p], recv_sem=hop_rsem.at[p],
            device_id={"segment": seg + step}, device_id_type=MESH,
        )

    def hop_sends(p):
        return jnp.logical_not(is_last) if p % 4 in (F0, B1) else jnp.logical_not(is_first)

    def hop_arrives(p):
        return jnp.logical_not(is_first) if p % 4 in (F0, B1) else jnp.logical_not(is_last)

    def out_copy(p):
        t, (forward, leg) = p // 4, ORDER[p % 4]
        return pltpu.make_async_copy(
            outs.at[p], (out_a_hbm if forward else out_g_hbm).at[t, leg], out_sem.at[p]
        )

    def rows_ref(p):
        forward, leg = ORDER[p % 4]
        return rows_in.at[2 * (p // 4) + (0 if forward else 1), leg]

    def enter(p):
        forward, leg = ORDER[p % 4]
        values = rows_ref(p)[...]
        gather[p, rows(me)] = normalize(values, gains[pl.ds(leg, 1), :]) if forward else values
        for d in range(1, n):
            ag_copy(p, d).start()

    def arrive(p):
        t, kind = p // 4, p % 4
        before = p - 4
        target = rows_ref(p)

        @pl.when(hop_arrives(before))
        def _():
            hop_copy(before).wait_recv()
            target[...] = hop[before]

        @pl.when(jnp.logical_not(hop_arrives(before)))
        def _():
            if kind == F0:
                target[...] = fresh[0, t - 1]
            elif kind == B1:
                target[...] = fresh[1, t - 1]
            elif kind == F1:
                target[...] = outs[before - F1 + F0]
            else:
                target[...] = outs[before - B0 + B1]

        enter(p)

    def scatter_one(p):
        for c in range(chips):
            s1_send[p, c] = acc[p % 2, rows(2 * c + (1 - core))].astype(jnp.bfloat16)
        s1_copy(p).start()

    def scatter_two(p):
        s1_copy(p).wait_recv()
        for d in range(1, chips):
            other = lax.rem(chip + d, chips)
            s2_send[p, d - 1] = (
                acc[p % 2, rows(2 * other + core)] + s1_recv[p, other].astype(jnp.float32)
            ).astype(jnp.bfloat16)
            s2_copy(p, d).start()
        acc[p % 2, rows(me)] += s1_recv[p, chip].astype(jnp.float32)

    def finish(p):
        t, (forward, leg) = p // 4, ORDER[p % 4]
        total = acc[p % 2, rows(me)]
        for d in range(1, chips):
            s2_copy(p, d).wait_recv()
            total = total + s2_recv[p, d - 1].astype(jnp.float32)
        entered = rows_ref(p)[...]
        if forward:
            outs[p] = (entered.astype(jnp.float32) + total).astype(jnp.bfloat16)
        else:
            outs[p] = norm_backward(entered, stash[t, leg], gains[pl.ds(leg, 1), :], total)
        out_copy(p).start()
        if t + 1 < ticks:
            @pl.when(hop_sends(p))
            def _():
                hop_copy(p).start()

    hooks = [[] for _ in range(passes + 1)]

    def at(p, eighth, call):
        hooks[min(p, passes)].append((min(eighth * tiles // 8, tiles - 1), eighth, call))

    at(0, 0, lambda: enter(B0))
    at(0, 4, lambda: (small[3].wait(), small[4].wait(), small[5].wait(), enter(B1)))
    at(1, 0, lambda: enter(F1))
    for p in range(passes):
        at(p + 1, 2, functools.partial(scatter_two, p))
        at(p + 1, 6, functools.partial(finish, p))
    for t in range(1, ticks):
        base = 4 * t
        at(base - 2, 4, functools.partial(arrive, base + F0))
        at(base - 1, 7, functools.partial(arrive, base + B0))
        at(base, 4, functools.partial(arrive, base + B1))
        at(base + 1, 4, functools.partial(arrive, base + F1))
    for entry in hooks:
        entry.sort(key=lambda item: item[1])

    small[0].wait()
    small[1].wait()
    enter(F0)
    small[2].wait()

    for p in range(passes):
        t, (forward, leg) = p // 4, ORDER[p % 4]
        first_use = t == 0 and p % 4 in (F0, B1)
        for d in range(1, n):
            ag_copy(p, d).wait_recv()
        acc[p % 2] = jnp.zeros_like(acc[p % 2])

        def step(i, carry, p=p, t=t, forward=forward, leg=leg, first_use=first_use):
            if p == 0:
                pre_copy(0, 0, i).start()
                for copy in w_copies(1, i):
                    copy.start()
                pre_copy(0, 1, i).start()
            if p % 4 == B0 and t + 1 < ticks:
                pre_copy(t + 1, 0, i).start()
                pre_copy(t + 1, 1, i).start()
            for where, _, call in hooks[p]:
                pl.when(i == where)(lambda call=call: (call(), None)[1])
            if first_use:
                for copy in w_copies(leg, i):
                    copy.wait()
            x = gather[p]
            if forward:
                hidden = jnp.maximum(jnp.dot(x, w_in[leg, i], preferred_element_type=jnp.float32), 0.0)
                acc[p % 2] += jnp.dot(hidden.astype(jnp.bfloat16), w_out[leg, i], preferred_element_type=jnp.float32)
            else:
                pre_copy(t, leg, i).wait()
                up = lax.dot_general(
                    x, w_out[leg, i], (((1,), (1,)), ((), ())), preferred_element_type=jnp.float32
                )
                masked = jnp.where(pre[2 * t + leg, i].astype(jnp.float32) > 0, up, 0.0).astype(jnp.bfloat16)
                acc[p % 2] += lax.dot_general(
                    masked, w_in[leg, i], (((1,), (1,)), ((), ())), preferred_element_type=jnp.float32
                )
            return carry

        lax.fori_loop(0, tiles, step, 0)
        scatter_one(p)

    for _, _, call in hooks[passes]:
        call()

    for p in range(passes):
        for d in range(1, n):
            ag_copy(p, d).wait_send()
        s1_copy(p).wait_send()
        for d in range(1, chips):
            s2_copy(p, d).wait_send()
        if p // 4 + 1 < ticks:
            @pl.when(hop_sends(p))
            def _():
                hop_copy(p).wait_send()
        out_copy(p).wait()


def body(n, sections, w_in, w_out, gains, acts, grads, fresh_a, fresh_g, stash, pre):
    ticks = stash.shape[0]
    _, legs, d, ff = w_in.shape
    r = acts.shape[3]
    total_rows = n * r
    tile = min(TILE, ff)
    tiles = ff // tile
    chips = n // 2
    passes = 4 * ticks
    bf16, f32 = jnp.bfloat16, jnp.float32
    any_spec = pl.BlockSpec(memory_space=pl.ANY)
    dma = pltpu.SemaphoreType.DMA
    far = max(chips - 1, 1)
    out = jax.ShapeDtypeStruct((ticks, legs, r, d), bf16)
    out_a, out_g = pl.pallas_call(
        functools.partial(kernel, n, sections, ticks, tiles, tile),
        out_shape=(out, out),
        in_specs=[any_spec] * 9,
        out_specs=(any_spec, any_spec),
        scratch_shapes=[
            pltpu.VMEM((legs, tiles, d, tile), bf16),
            pltpu.VMEM((legs, tiles, tile, d), bf16),
            pltpu.VMEM((ticks * legs, tiles, total_rows, tile), bf16),
            pltpu.VMEM((legs, d), f32),
            pltpu.VMEM((2 * ticks, legs, r, d), bf16),
            pltpu.VMEM((2,) + (max(ticks - 1, 1), r, d), bf16),
            pltpu.VMEM((ticks, legs, r, d), bf16),
            pltpu.VMEM((passes, total_rows, d), bf16),
            pltpu.VMEM((2, total_rows, d), f32),
            pltpu.VMEM((passes, chips, r, d), bf16),
            pltpu.VMEM((passes, chips, r, d), bf16),
            pltpu.VMEM((passes, far, r, d), bf16),
            pltpu.VMEM((passes, far, r, d), bf16),
            pltpu.VMEM((passes, r, d), bf16),
            pltpu.VMEM((passes, r, d), bf16),
            dma((2, legs, tiles)),
            dma((ticks * legs, tiles)),
            dma((6,)),
            dma((passes, n - 1)),
            dma((passes, n - 1)),
            dma((passes,)),
            dma((passes,)),
            dma((passes, far)),
            dma((passes, far)),
            dma((passes,)),
            dma((passes,)),
            dma((passes,)),
        ],
        compiler_params=pltpu.CompilerParams(
            collective_id=0, has_side_effects=True, vmem_limit_bytes=67043328
        ),
        name="relay",
    )(
        w_in[0], w_out[0], gains[0], acts[0, :, 0], grads[0, :, 0],
        fresh_a[:, 0], fresh_g[:, 0], stash[:, 0, :, 0], pre[:, 0, :, 0],
    )
    return out_a[:, None, :, None], out_g[:, None, :, None]


def solution(mesh):
    return jax.shard_map(
        functools.partial(body, mesh.shape["mp"], mesh.shape["segment"]),
        mesh=mesh,
        in_specs=(
            P("segment", None, None, "mp"),
            P("segment", None, "mp", None),
            P("segment", None, None),
            P("segment", None, "tok", "mp", None),
            P("segment", None, "tok", "mp", None),
            P(None, "tok", "mp", None),
            P(None, "tok", "mp", None),
            P(None, "segment", None, "tok", "mp", None),
            P(None, "segment", None, "tok", None, "mp"),
        ),
        out_specs=(
            P(None, "segment", None, "tok", "mp", None),
            P(None, "segment", None, "tok", "mp", None),
        ),
        check_vma=False,
    )
```

```python
import functools

import jax
import jax.numpy as jnp
from jax import lax
from jax.experimental import pallas as pl
from jax.experimental.pallas import tpu as pltpu
from jax.sharding import PartitionSpec as P

MESH = pl.DeviceIdType.MESH
EPS = 1e-06
TILE = 2048
S_TWO = 2
S_FIN = 8
ARRIVE = (22, 32, 38, 46)
ORDER = ((True, 0), (False, 0), (False, 1), (True, 1))
F0, B0, B1, F1 = range(4)


def normalize(values, gain_row):
    wide = values.astype(jnp.float32)
    inverse = lax.rsqrt(jnp.mean(wide * wide, axis=-1, keepdims=True) + EPS)
    return (wide * inverse * gain_row).astype(jnp.bfloat16)


def norm_backward(gradient, stashed, gain_row, norm_grad):
    wide = stashed.astype(jnp.float32)
    inverse = lax.rsqrt(jnp.mean(wide * wide, axis=-1, keepdims=True) + EPS)
    scaled = gain_row * norm_grad
    inner = jnp.mean(wide * scaled, axis=-1, keepdims=True)
    result = gradient.astype(jnp.float32) + inverse * scaled - wide * (inverse * inverse * inverse * inner)
    return result.astype(jnp.bfloat16)


def kernel(
    n, sections, ticks, tiles, tile,
    w_in_hbm, w_out_hbm, gains_hbm, acts_hbm, grads_hbm, fresh_a_hbm, fresh_g_hbm, stash_hbm, pre_hbm,
    out_a_hbm, out_g_hbm,
    w_in, w_out, pre, gains, rows_in, fresh, stash,
    gather, acc, own, s1_send, s1_recv, s2_send, s2_recv, outs, hop,
    w_sem, pre_sem, small_sem, far_ssem, far_rsem, near_ssem, near_rsem, s1_ssem, s1_rsem, s2_ssem, s2_rsem, hop_ssem, hop_rsem, out_sem,
):
    me = lax.axis_index("mp")
    seg = lax.axis_index("segment")
    core = lax.rem(me, 2)
    chip = me // 2
    chips = n // 2
    partner = chip * 2 + (1 - core)
    is_first = seg == 0
    is_last = seg == sections - 1
    r = rows_in.shape[2]
    passes = 4 * ticks

    def rows(block):
        return pl.ds(pl.multiple_of(block * r, r), r)

    small = [
        pltpu.make_async_copy(acts_hbm, rows_in.at[0], small_sem.at[0]),
        pltpu.make_async_copy(gains_hbm, gains, small_sem.at[1]),
        pltpu.make_async_copy(grads_hbm, rows_in.at[1], small_sem.at[2]),
        pltpu.make_async_copy(stash_hbm, stash, small_sem.at[3]),
        pltpu.make_async_copy(fresh_a_hbm, fresh.at[0], small_sem.at[4]),
        pltpu.make_async_copy(fresh_g_hbm, fresh.at[1], small_sem.at[5]),
    ]

    def w_copies(leg, i):
        cut = pl.ds(pl.multiple_of(i * tile, tile), tile)
        return (
            pltpu.make_async_copy(w_in_hbm.at[leg, :, cut], w_in.at[leg, i], w_sem.at[0, leg, i]),
            pltpu.make_async_copy(w_out_hbm.at[leg, cut, :], w_out.at[leg, i], w_sem.at[1, leg, i]),
        )

    def pre_copy(t, leg, i):
        cut = pl.ds(pl.multiple_of(i * tile, tile), tile)
        return pltpu.make_async_copy(pre_hbm.at[t, leg, :, cut], pre.at[2 * t + leg, i], pre_sem.at[2 * t + leg, i])

    small[0].start()
    small[1].start()
    small[2].start()
    for copy in w_copies(0, 0):
        copy.start()
    for copy in small[3:]:
        copy.start()

    barrier = pltpu.get_barrier_semaphore()
    for d in range(1, n):
        pl.semaphore_signal(barrier, inc=1, device_id={"mp": lax.rem(me + d, n)}, device_id_type=MESH)

    @pl.when(seg > 0)
    def _():
        pl.semaphore_signal(barrier, inc=1, device_id={"segment": seg - 1}, device_id_type=MESH)

    @pl.when(seg < sections - 1)
    def _():
        pl.semaphore_signal(barrier, inc=1, device_id={"segment": seg + 1}, device_id_type=MESH)

    peers = n - 1 + (seg > 0).astype(jnp.int32) + (seg < sections - 1).astype(jnp.int32)
    pl.semaphore_wait(barrier, peers)

    def far_copy(p, d):
        return pltpu.make_async_remote_copy(
            src_ref=gather.at[p, rows(me)], dst_ref=gather.at[p, rows(me)],
            send_sem=far_ssem.at[p, d - 1], recv_sem=far_rsem.at[p, d - 1],
            device_id={"mp": lax.rem(chip + d, chips) * 2 + core}, device_id_type=MESH,
        )

    def near_copy(p, d):
        block = lax.rem(chip + chips - d, chips) * 2 + core
        return pltpu.make_async_remote_copy(
            src_ref=gather.at[p, rows(block)], dst_ref=gather.at[p, rows(block)],
            send_sem=near_ssem.at[p, d], recv_sem=near_rsem.at[p, d],
            device_id={"mp": partner}, device_id_type=MESH,
        )

    def s1_copy(p):
        return pltpu.make_async_remote_copy(
            src_ref=s1_send.at[p], dst_ref=s1_recv.at[p],
            send_sem=s1_ssem.at[p], recv_sem=s1_rsem.at[p],
            device_id={"mp": partner}, device_id_type=MESH,
        )

    def s2_copy(p, d):
        return pltpu.make_async_remote_copy(
            src_ref=s2_send.at[p, d - 1], dst_ref=s2_recv.at[p, d - 1],
            send_sem=s2_ssem.at[p, d - 1], recv_sem=s2_rsem.at[p, d - 1],
            device_id={"mp": lax.rem(chip + d, chips) * 2 + core}, device_id_type=MESH,
        )

    def hop_copy(p):
        step = 1 if p % 4 in (F0, B1) else -1
        return pltpu.make_async_remote_copy(
            src_ref=outs.at[p], dst_ref=hop.at[p],
            send_sem=hop_ssem.at[p], recv_sem=hop_rsem.at[p],
            device_id={"segment": seg + step}, device_id_type=MESH,
        )

    def hop_sends(p):
        return jnp.logical_not(is_last) if p % 4 in (F0, B1) else jnp.logical_not(is_first)

    def hop_arrives(p):
        return jnp.logical_not(is_first) if p % 4 in (F0, B1) else jnp.logical_not(is_last)

    def out_copy(p):
        t, (forward, leg) = p // 4, ORDER[p % 4]
        return pltpu.make_async_copy(
            outs.at[p], (out_a_hbm if forward else out_g_hbm).at[t, leg], out_sem.at[p]
        )

    def rows_ref(p):
        forward, leg = ORDER[p % 4]
        return rows_in.at[2 * (p // 4) + (0 if forward else 1), leg]

    def enter(p):
        forward, leg = ORDER[p % 4]
        values = rows_ref(p)[...]
        gather[p, rows(me)] = normalize(values, gains[pl.ds(leg, 1), :]) if forward else values
        for d in range(1, chips):
            far_copy(p, d).start()
        near_copy(p, 0).start()

    def relay(p):
        for d in range(1, chips):
            far_copy(p, d).wait_recv()
            near_copy(p, d).start()

    def arrive(p):
        t, kind = p // 4, p % 4
        before = p - 4
        target = rows_ref(p)

        @pl.when(hop_arrives(before))
        def _():
            hop_copy(before).wait_recv()
            target[...] = hop[before]

        @pl.when(jnp.logical_not(hop_arrives(before)))
        def _():
            if kind == F0:
                target[...] = fresh[0, t - 1]
            elif kind == B1:
                target[...] = fresh[1, t - 1]
            elif kind == F1:
                target[...] = outs[before - F1 + F0]
            else:
                target[...] = outs[before - B0 + B1]

        enter(p)

    def scatter_one(p):
        for c in range(chips):
            s1_send[p, c] = acc[p % 2, rows(2 * c + (1 - core))].astype(jnp.bfloat16)
        s1_copy(p).start()

    def scatter_two(p):
        s1_copy(p).wait_recv()
        for d in range(1, chips):
            other = lax.rem(chip + d, chips)
            s2_send[p, d - 1] = (
                acc[p % 2, rows(2 * other + core)] + s1_recv[p, other].astype(jnp.float32)
            ).astype(jnp.bfloat16)
            s2_copy(p, d).start()
        own[p] = acc[p % 2, rows(me)] + s1_recv[p, chip].astype(jnp.float32)

    def finish(p):
        t, (forward, leg) = p // 4, ORDER[p % 4]
        total = own[p]
        for d in range(1, chips):
            s2_copy(p, d).wait_recv()
            total = total + s2_recv[p, d - 1].astype(jnp.float32)
        entered = rows_ref(p)[...]
        if forward:
            outs[p] = (entered.astype(jnp.float32) + total).astype(jnp.bfloat16)
        else:
            outs[p] = norm_backward(entered, stash[t, leg], gains[pl.ds(leg, 1), :], total)
        out_copy(p).start()
        if t + 1 < ticks:
            @pl.when(hop_sends(p))
            def _():
                hop_copy(p).start()

    hooks = [[] for _ in range(passes + 1)]
    order = []

    def at(p, eighth, call):
        key = (8 * p + eighth, len(order))
        order.append(key)
        hooks[min(p, passes)].append((min(eighth * tiles // 8, tiles - 1), key, call))

    at(0, 4, lambda: (small[3].wait(), small[4].wait(), small[5].wait(), enter(B1)))
    at(0, 6, lambda: relay(B0))
    at(1, 0, lambda: enter(F1))
    at(1, 2, lambda: relay(B1))
    at(1, 6, lambda: relay(F1))
    for p in range(passes):
        at(p + 1, S_TWO, functools.partial(scatter_two, p))
        at(p + 1 + S_FIN // 8, S_FIN % 8, functools.partial(finish, p))
    for t in range(1, ticks):
        for kind in range(4):
            slot = ARRIVE[kind]
            at(4 * t - 4 + slot // 8, slot % 8, functools.partial(arrive, 4 * t + kind))
            at(4 * t - 4 + (slot + 6) // 8, (slot + 6) % 8, functools.partial(relay, 4 * t + kind))
    for entry in hooks:
        entry.sort(key=lambda item: item[1])

    small[0].wait()
    small[1].wait()
    enter(F0)
    for i in range(1, tiles):
        for copy in w_copies(0, i):
            copy.start()
    for i in range(tiles):
        pre_copy(0, 0, i).start()
    for i in range(tiles):
        pre_copy(0, 1, i).start()
        for copy in w_copies(1, i):
            copy.start()
    relay(F0)
    small[2].wait()
    enter(B0)

    for p in range(passes):
        t, (forward, leg) = p // 4, ORDER[p % 4]
        first_use = t == 0 and p % 4 in (F0, B1)
        for d in range(chips):
            near_copy(p, d).wait_recv()
        acc[p % 2] = jnp.zeros_like(acc[p % 2])

        def step(i, carry, p=p, t=t, forward=forward, leg=leg, first_use=first_use):
            if p % 4 == B0 and t + 1 < ticks:
                pre_copy(t + 1, 0, i).start()
                pre_copy(t + 1, 1, i).start()
            for where, _, call in hooks[p]:
                pl.when(i == where)(lambda call=call: (call(), None)[1])
            if first_use:
                for copy in w_copies(leg, i):
                    copy.wait()
            x = gather[p]
            if forward:
                hidden = jnp.maximum(jnp.dot(x, w_in[leg, i], preferred_element_type=jnp.float32), 0.0)
                acc[p % 2] += jnp.dot(hidden.astype(jnp.bfloat16), w_out[leg, i], preferred_element_type=jnp.float32)
            else:
                pre_copy(t, leg, i).wait()
                up = lax.dot_general(
                    x, w_out[leg, i], (((1,), (1,)), ((), ())), preferred_element_type=jnp.float32
                )
                masked = jnp.where(pre[2 * t + leg, i].astype(jnp.float32) > 0, up, 0.0).astype(jnp.bfloat16)
                acc[p % 2] += lax.dot_general(
                    masked, w_in[leg, i], (((1,), (1,)), ((), ())), preferred_element_type=jnp.float32
                )
            return carry

        lax.fori_loop(0, tiles, step, 0)
        scatter_one(p)

    for _, _, call in hooks[passes]:
        call()

    for p in range(passes):
        for d in range(1, chips):
            far_copy(p, d).wait_send()
        for d in range(chips):
            near_copy(p, d).wait_send()
        s1_copy(p).wait_send()
        for d in range(1, chips):
            s2_copy(p, d).wait_send()
        if p // 4 + 1 < ticks:
            @pl.when(hop_sends(p))
            def _():
                hop_copy(p).wait_send()
        out_copy(p).wait()


def flush(a_ref, g_ref, out_a_ref, out_g_ref, held, sem):
    pairs = ((a_ref, out_a_ref), (g_ref, out_g_ref))
    loads = [pltpu.make_async_copy(src, held.at[k], sem.at[0, k]) for k, (src, _) in enumerate(pairs)]
    stores = [pltpu.make_async_copy(held.at[k], dst, sem.at[1, k]) for k, (_, dst) in enumerate(pairs)]
    for copy in loads:
        copy.start()
    for load, store in zip(loads, stores):
        load.wait()
        store.start()
    for copy in stores:
        copy.wait()


def body(n, sections, w_in, w_out, gains, acts, grads, fresh_a, fresh_g, stash, pre):
    ticks = stash.shape[0]
    _, legs, d, ff = w_in.shape
    r = acts.shape[3]
    total_rows = n * r
    tile = min(TILE, ff)
    tiles = ff // tile
    chips = n // 2
    passes = 4 * ticks
    bf16, f32 = jnp.bfloat16, jnp.float32
    any_spec = pl.BlockSpec(memory_space=pl.ANY)
    dma = pltpu.SemaphoreType.DMA
    far = max(chips - 1, 1)
    out = jax.ShapeDtypeStruct((ticks, legs, r, d), bf16)
    out_a, out_g = pl.pallas_call(
        functools.partial(kernel, n, sections, ticks, tiles, tile),
        out_shape=(out, out),
        in_specs=[any_spec] * 9,
        out_specs=(any_spec, any_spec),
        scratch_shapes=[
            pltpu.VMEM((legs, tiles, d, tile), bf16),
            pltpu.VMEM((legs, tiles, tile, d), bf16),
            pltpu.VMEM((ticks * legs, tiles, total_rows, tile), bf16),
            pltpu.VMEM((legs, d), f32),
            pltpu.VMEM((2 * ticks, legs, r, d), bf16),
            pltpu.VMEM((2,) + (max(ticks - 1, 1), r, d), bf16),
            pltpu.VMEM((ticks, legs, r, d), bf16),
            pltpu.VMEM((passes, total_rows, d), bf16),
            pltpu.VMEM((2, total_rows, d), f32),
            pltpu.VMEM((passes, r, d), f32),
            pltpu.VMEM((passes, chips, r, d), bf16),
            pltpu.VMEM((passes, chips, r, d), bf16),
            pltpu.VMEM((passes, far, r, d), bf16),
            pltpu.VMEM((passes, far, r, d), bf16),
            pltpu.VMEM((passes, r, d), bf16),
            pltpu.VMEM((passes, r, d), bf16),
            dma((2, legs, tiles)),
            dma((ticks * legs, tiles)),
            dma((6,)),
            dma((passes, far)),
            dma((passes, far)),
            dma((passes, chips)),
            dma((passes, chips)),
            dma((passes,)),
            dma((passes,)),
            dma((passes, far)),
            dma((passes, far)),
            dma((passes,)),
            dma((passes,)),
            dma((passes,)),
        ],
        compiler_params=pltpu.CompilerParams(
            collective_id=0, has_side_effects=True, vmem_limit_bytes=67043328
        ),
        name="relay",
    )(
        w_in[0], w_out[0], gains[0], acts[0, :, 0], grads[0, :, 0],
        fresh_a[:, 0], fresh_g[:, 0], stash[:, 0, :, 0], pre[:, 0, :, 0],
    )
    out_a, out_g = pl.pallas_call(
        flush,
        out_shape=(out, out),
        in_specs=[any_spec] * 2,
        out_specs=(any_spec, any_spec),
        scratch_shapes=[pltpu.VMEM((2,) + out.shape, bf16), dma((2, 2))],
        name="flush",
    )(out_a, out_g)
    return out_a[:, None, :, None], out_g[:, None, :, None]


def solution(mesh):
    return jax.shard_map(
        functools.partial(body, mesh.shape["mp"], mesh.shape["segment"]),
        mesh=mesh,
        in_specs=(
            P("segment", None, None, "mp"),
            P("segment", None, "mp", None),
            P("segment", None, None),
            P("segment", None, "tok", "mp", None),
            P("segment", None, "tok", "mp", None),
            P(None, "tok", "mp", None),
            P(None, "tok", "mp", None),
            P(None, "segment", None, "tok", "mp", None),
            P(None, "segment", None, "tok", None, "mp"),
        ),
        out_specs=(
            P(None, "segment", None, "tok", "mp", None),
            P(None, "segment", None, "tok", "mp", None),
        ),
        check_vma=False,
    )
```
